256 devices in a mesh: row: 16 (over y, z_hi, core), col: 16 (over x, z_lo).
Axes of the slice: x: 4, y: 4, z: 8 (z_hi: 2, z_lo: 4; z = z_hi * 4 + z_lo), core: 2. Of those that a mesh axis runs over, the one named last changes fastest.
Arguments:
- vectors: bfloat16 [16, 131072], P(None, ('row', 'col')), may hold values from -6 to 6
- tiles: bfloat16 [16, 16, 1024, 4096], P('row', 'col'), may hold values from -0.0625 to 0.0625
- tile_rows: int32 [16, 16, 1024], P('row', 'col'), may hold values from 0 to 127
- tile_cols: int32 [16, 16, 1024], P('row', 'col'), may hold values from 0 to 127
- tile_counts: int32 [16, 16], P('row', 'col'), may hold values from 128 to 1024, as said below
Outputs:
- applied: float32 [16, 131072], P(None, ('row', 'col'))
The draws below stay inside these ranges and needn't reach their ends.
Inputs may be any that keep to these rules, and one draw needn't show every extreme that they name: `tile_counts`: every cell has 128, 256, 512 or 1024 live slots, and some cell has 1024.
All inputs are finite; a program needn't handle non-finite values.
Results may differ from the reference program's by a relative error of at most 0.0003.
Values may be sent and summed in bfloat16 or wider, within the bound.
A program may use at most 128 MiB of HBM per device.

```python
import jax
import jax.numpy as jnp
from jax import lax

NV = 16
TILE = 64
P_SIZE = 512
MAXT = 1024
DIM = 131072
ROW_TILES = 128
COL_TILES = 128
N_ROW = 16
N_COL = 16


def draw_tile_counts(key, part):
    levels = jax.random.randint(key, (N_ROW * N_COL,), 0, 4)
    counts = jnp.right_shift(jnp.full((N_ROW * N_COL,), MAXT, jnp.int32), levels.astype(jnp.int32))
    fullest = jax.random.randint(jax.random.fold_in(key, 7), (), 0, N_ROW * N_COL)
    counts = counts.at[fullest].set(MAXT)
    return counts.reshape(N_ROW, N_COL).astype(jnp.int32)


def touch_ends(array, rng, smallest, high):
    dims = array.shape
    index_at = [jax.random.randint(jax.random.fold_in(rng, axis), (), 0, dims[axis]) for axis in range(len(dims))]
    array = array.at[tuple(index_at)].set(smallest)
    longest = dims.index(max(dims))
    index_at[longest] = (index_at[longest] + 1) % dims[longest]
    return array.at[tuple(index_at)].set(high)


def block_levels(own_key, dims, split, low, largest):
    def one(axis_at, shards_of):
        steps = jax.random.uniform(jax.random.fold_in(jax.random.fold_in(own_key, 6), axis_at), (shards_of,), jnp.float32, low / len(split), largest / len(split))
        return jnp.repeat(jnp.exp(steps), dims[axis_at] // shards_of).reshape((-1,) + (1,) * (len(dims) - axis_at - 1))

    level = one(*split[0])
    for cut in split[1:]:
        level = level * one(*cut)
    return level


def centred(key, dims, width, most, pieces=(), held_as=jnp.bfloat16):
    drawn = width * jax.random.normal(key, dims, jnp.float32)
    if pieces:
        drawn = drawn * block_levels(key, dims, pieces, -0.22, 0.18)
    return jnp.clip(drawn, -most, most).astype(held_as)


def setup_inputs(seed: int = 0) -> dict:
    key_of = jax.random.split(jax.random.key(seed), 6)
    return {
        "vectors": centred(key_of[0], (NV, DIM), 1.0, 6.0, ((1, 256),)),
        "tiles": centred(key_of[1], (N_ROW, N_COL, MAXT, TILE * TILE), (max(TILE * TILE * MAXT // P_SIZE, 1)) ** -0.5, 0.0625, ((0, 16), (1, 16))),
        "tile_rows": touch_ends(jax.random.randint(key_of[2], (N_ROW, N_COL, MAXT), 0, ROW_TILES), jax.random.fold_in(key_of[2], 1), 0, ROW_TILES - 1).astype(jnp.int32),
        "tile_cols": touch_ends(jax.random.randint(key_of[3], (N_ROW, N_COL, MAXT), 0, COL_TILES), jax.random.fold_in(key_of[3], 1), 0, COL_TILES - 1).astype(jnp.int32),
        "tile_counts": draw_tile_counts(jax.random.fold_in(key_of[5], 71), 0),
    }


def reference(vectors, tiles, tile_rows, tile_cols, tile_counts):
    cells = N_ROW * N_COL
    blocks = tiles.reshape(cells, MAXT, TILE, TILE)
    row_ids = tile_rows.reshape(cells, MAXT)
    col_ids = tile_cols.reshape(cells, MAXT)
    live_counts = tile_counts.reshape(cells)
    spread = vectors.reshape(NV, N_ROW, N_COL, P_SIZE)

    def visit(totals, device):
        forward_acc, transposed_acc = totals
        grid_row = device // N_COL
        grid_col = device % N_COL
        segment = lax.dynamic_index_in_dim(spread, grid_row, 1, keepdims=False).reshape(NV, ROW_TILES, TILE)
        col_set = lax.dynamic_index_in_dim(spread, grid_col, 2, keepdims=False).reshape(NV, COL_TILES, TILE)
        blocks_now = lax.dynamic_index_in_dim(blocks, device, 0, keepdims=False)
        rows_now = lax.dynamic_index_in_dim(row_ids, device, 0, keepdims=False)
        cols_now = lax.dynamic_index_in_dim(col_ids, device, 0, keepdims=False)
        is_live = jnp.arange(MAXT, dtype=jnp.int32) < live_counts[device]
        blocks_now = jnp.where(is_live[:, None, None], blocks_now.astype(jnp.float32), jnp.float32(0.0))
        col_pick = col_set[:, cols_now].astype(jnp.float32)
        row_pick = segment[:, rows_now].astype(jnp.float32)
        forward = jnp.einsum("vtj,tij->tvi", col_pick, blocks_now, precision=lax.Precision.HIGHEST).reshape(MAXT, NV * TILE)
        transposed = jnp.einsum("vti,tij->tvj", row_pick, blocks_now, precision=lax.Precision.HIGHEST).reshape(MAXT, NV * TILE)
        forward_rows = jax.ops.segment_sum(forward, rows_now, num_segments=ROW_TILES)
        transposed_cols = jax.ops.segment_sum(transposed, cols_now, num_segments=COL_TILES)
        forward_acc = forward_acc.at[grid_row].add(forward_rows)
        transposed_acc = transposed_acc.at[grid_col].add(transposed_cols)
        return (forward_acc, transposed_acc), None

    start = (jnp.zeros((N_ROW, ROW_TILES, NV * TILE), jnp.float32), jnp.zeros((N_COL, COL_TILES, NV * TILE), jnp.float32))
    (forward_acc, transposed_acc), _ = lax.scan(visit, start, jnp.arange(cells, dtype=jnp.int32))
    forward_full = forward_acc.reshape(N_ROW, ROW_TILES, NV, TILE).transpose(2, 0, 1, 3).reshape(NV, DIM)
    transposed_full = transposed_acc.reshape(N_COL, COL_TILES, NV, TILE).transpose(2, 0, 1, 3)
    transposed_full = transposed_full.reshape(NV, N_COL, N_ROW, P_SIZE).transpose(0, 2, 1, 3).reshape(NV, DIM)
    return forward_full + transposed_full
```

```python
import functools

import jax
import jax.numpy as jnp
from jax import lax
from jax.experimental import pallas as pl
from jax.experimental.pallas import tpu as pltpu
from jax.sharding import PartitionSpec as P

MESH = pl.DeviceIdType.MESH


class Place:
    def __init__(self):
        self.a, self.b = lax.axis_index("row"), lax.axis_index("col")
        self.y, self.h, self.k = self.a // 4, (self.a // 2) % 2, self.a % 2
        self.x, self.z = self.b // 4, self.b % 4

    def row(self, dy=0, dh=0, dk=0):
        return ((self.y + dy) % 4) * 4 + ((self.h + dh) % 2) * 2 + (self.k + dk) % 2

    def col(self, dx=0, dz=0):
        return ((self.x + dx) % 4) * 4 + (self.z + dz) % 4

    def meet(self):
        peers = [(self.row(dh=1), self.b), (self.row(dk=1), self.b)]
        peers += [(self.row(dy=d), self.b) for d in (1, 2, 3)]
        peers += [(self.a, self.col(dx=d)) for d in (1, 2, 3)]
        peers += [(self.a, self.col(dz=d)) for d in (1, 2, 3)]
        barrier = pltpu.get_barrier_semaphore()
        for peer in peers:
            pl.semaphore_signal(barrier, inc=1, device_id=peer, device_id_type=MESH)
        pl.semaphore_wait(barrier, len(peers))


class Sends:
    def __init__(self, sems):
        self.sems, self.started = sems, []

    def go(self, src, dst, recv_sem, device):
        copy = pltpu.make_async_remote_copy(
            src_ref=src, dst_ref=dst, send_sem=self.sems.at[len(self.started)],
            recv_sem=recv_sem, device_id=device, device_id_type=MESH)
        copy.start()
        self.started.append(copy)

    def arrived(self, dst, recv_sem, device):
        pltpu.make_async_remote_copy(
            src_ref=dst, dst_ref=dst, send_sem=self.sems.at[0],
            recv_sem=recv_sem, device_id=device, device_id_type=MESH).wait_recv()

    def finish(self):
        for copy in self.started:
            copy.wait_send()


def gather_kernel(vec, row_set, col_set, send_sems, row_sems, col_sems):
    at = Place()
    a, b = at.a, at.b
    sends = Sends(send_sems)
    at.meet()
    mine_r, mine_c = row_set.at[b], col_set.at[a]
    sends.go(vec, mine_c, col_sems.at[a], (at.row(dh=1), b))
    for d in (2, 1, 3):
        sends.go(vec, mine_r, row_sems.at[b], (a, at.col(dz=d)))
    for d in (2, 1, 3):
        sends.go(vec, mine_c, col_sems.at[a], (at.row(dy=d), b))
    for d in (2, 1, 3):
        sends.go(vec, mine_r, row_sems.at[b], (a, at.col(dx=d)))
    sends.go(vec, mine_c, col_sems.at[a], (at.row(dk=1), b))
    row_set[b] = vec[...]
    col_set[a] = vec[...]

    def got_r(j):
        sends.arrived(row_set.at[j], row_sems.at[j], (a, b))

    def got_c(j):
        sends.arrived(col_set.at[j], col_sems.at[j], (a, b))

    for d in (1, 3, 2):
        j = at.col(dz=d)
        got_r(j)
        for e in (2, 1, 3):
            sends.go(row_set.at[j], row_set.at[j], row_sems.at[j], (a, at.col(dx=e)))
    j = at.row(dh=1)
    got_c(j)
    for e in (2, 1, 3):
        sends.go(col_set.at[j], col_set.at[j], col_sems.at[j], (at.row(dy=e), b))
    sends.go(col_set.at[j], col_set.at[j], col_sems.at[j], (at.row(dk=1), b))
    for dh in (0, 1):
        for d in (1, 3, 2):
            j = at.row(dy=d, dh=dh)
            got_c(j)
            sends.go(col_set.at[j], col_set.at[j], col_sems.at[j], (at.row(dk=1), b))
    for dh in (0, 1):
        for d in (0, 1, 2, 3):
            got_c(at.row(dy=d, dh=dh, dk=1))
    for d in (1, 3, 2):
        for e in (0, 1, 3, 2):
            got_r(at.col(dx=d, dz=e))
    sends.finish()


def gather(vectors):
    whole = jax.ShapeDtypeStruct((16,) + vectors.shape, vectors.dtype)
    vmem = pl.BlockSpec(memory_space=pltpu.VMEM)
    return pl.pallas_call(
        gather_kernel,
        out_shape=(whole, whole),
        in_specs=[vmem],
        out_specs=(vmem, vmem),
        scratch_shapes=[
            pltpu.SemaphoreType.DMA((30,)),
            pltpu.SemaphoreType.DMA((16,)),
            pltpu.SemaphoreType.DMA((16,)),
        ],
        compiler_params=pltpu.CompilerParams(collective_id=0, has_side_effects=True),
        name="gather",
    )(vectors)


def scatter_kernel(f, c, out, fx, fs, fz, cc, cs, cy, ch, send_sems, fx_sems, fz_sems, cc_sems, cy_sems, ch_sem):
    at = Place()
    a, b = at.a, at.b
    sends = Sends(send_sems)
    at.meet()
    far = (2, 1, 3)
    for dy in (2, 1, 3, 0):
        for dh in (1, 0):
            n = dy * 2 + dh
            sends.go(c.at[at.row(dy=dy, dh=dh, dk=1)], cc.at[n], cc_sems.at[n], (at.row(dk=1), b))
    for dz in (2, 1, 3, 0):
        for dx in far:
            n = dz * 3 + dx - 1
            sends.go(f.at[at.col(dx=dx, dz=dz)], fx.at[n], fx_sems.at[n], (a, at.col(dx=dx)))

    def sum_core(dy, dh):
        n = dy * 2 + dh
        sends.arrived(cc.at[n], cc_sems.at[n], (a, b))
        cs[n] = c[at.row(dy=dy, dh=dh)] + cc[n]

    def sum_x(dz):
        for dx in far:
            n = dz * 3 + dx - 1
            sends.arrived(fx.at[n], fx_sems.at[n], (a, b))
        fs[dz] = (f[at.col(dz=dz)] + fx[dz * 3]) + (fx[dz * 3 + 1] + fx[dz * 3 + 2])

    def sum_y(dh):
        for dy in far:
            n = (dy - 1) * 2 + dh
            sends.arrived(cy.at[n], cy_sems.at[n], (a, b))
        cs[dh] = (cs[dh] + cy[dh]) + (cy[2 + dh] + cy[4 + dh])

    for dy in far:
        for dh in (1, 0):
            sum_core(dy, dh)
            n = (dy - 1) * 2 + dh
            sends.go(cs.at[dy * 2 + dh], cy.at[n], cy_sems.at[n], (at.row(dy=dy), b))
    sum_core(0, 1)
    sum_core(0, 0)
    for dz in far:
        sum_x(dz)
        sends.go(fs.at[dz], fz.at[dz - 1], fz_sems.at[dz - 1], (a, at.col(dz=dz)))
        if dz == 2:
            sum_y(1)
            sends.go(cs.at[1], ch, ch_sem, (at.row(dh=1), b))
    sum_y(0)
    sum_x(0)
    sends.arrived(ch, ch_sem, (a, b))
    total = fs[0] + (cs[0] + ch[...])
    for dz in (1, 3, 2):
        sends.arrived(fz.at[dz - 1], fz_sems.at[dz - 1], (a, b))
    out[...] = total + (fz[0] + (fz[1] + fz[2]))
    sends.finish()


def scatter(f, c):
    block = f.shape[1:]
    vmem = pl.BlockSpec(memory_space=pltpu.VMEM)

    def room(n):
        return pltpu.VMEM((n,) + block, jnp.float32)

    return pl.pallas_call(
        scatter_kernel,
        out_shape=jax.ShapeDtypeStruct(block, jnp.float32),
        in_specs=[vmem, vmem],
        out_specs=vmem,
        scratch_shapes=[
            room(12), room(4), room(3), room(8), room(8), room(6), pltpu.VMEM(block, jnp.float32),
            pltpu.SemaphoreType.DMA((30,)),
            pltpu.SemaphoreType.DMA((12,)),
            pltpu.SemaphoreType.DMA((3,)),
            pltpu.SemaphoreType.DMA((8,)),
            pltpu.SemaphoreType.DMA((6,)),
            pltpu.SemaphoreType.DMA,
        ],
        compiler_params=pltpu.CompilerParams(collective_id=1, has_side_effects=True),
        name="scatter",
    )(f, c)


def lane_low(shape):
    return lax.broadcasted_iota(jnp.int32, shape, 1) < 64

def halves(v):
    lo, hi = v[:, :64], v[:, 64:]
    return jnp.concatenate([lo, lo], axis=1), jnp.concatenate([hi, hi], axis=1)

def local_kernel(copies, rows, cols, count, row_set, col_set, tiles, f_out, c_out, *scratch):
    tbuf, tsem, x2r, x2c = scratch[:4]
    stages = scratch[4:6]
    f_acc = scratch[6:6 + 2 * copies]
    c_acc = scratch[6 + 2 * copies:6 + 4 * copies]
    chunks = count[0] // 32

    def fetch(k):
        at = pl.ds(pl.multiple_of(k * 32, 32), 32)
        return pltpu.make_async_copy(tiles.at[at, :], tbuf.at[at, :], tsem.at[k])

    @pl.loop(0, chunks)
    def _(k):
        fetch(k).start()

    @pl.loop(0, 128)
    def _(r):
        for acc in f_acc + c_acc:
            acc[r] = jnp.zeros((16, 128), jnp.float32)

    @pl.loop(0, 16)
    def _(b):
        for src, dst in ((row_set, x2r), (col_set, x2c)):
            for t in range(4):
                lo, hi = halves(src[b, :, t * 128:(t + 1) * 128])
                dst[b * 8 + 2 * t] = lo
                dst[b * 8 + 2 * t + 1] = hi

    def relayout(slot, stage):
        for p in range(32):
            v0 = tbuf[pl.ds(pl.multiple_of(slot * 32, 32), 16), p * 128:(p + 1) * 128]
            v1 = tbuf[pl.ds(pl.multiple_of(slot * 32 + 16, 16), 16), p * 128:(p + 1) * 128]
            even = jnp.concatenate([v0[:, :64], v1[:, :64]], axis=1)
            odd = jnp.concatenate([v0[:, 64:], v1[:, 64:]], axis=1)
            stage[pl.ds(32 * p, 16), :] = even.astype(jnp.float32)
            stage[pl.ds(32 * p + 16, 16), :] = odd.astype(jnp.float32)

    def compute(base, stage):
        low = lane_low((16, 128))
        lowu = lane_low((64, 128))
        for s in range(16):
            u = stage[pl.ds(s, 64, stride=16), :].astype(jnp.bfloat16)
            zero = jnp.zeros_like(u)
            bd = jnp.concatenate([jnp.where(lowu, u, zero), jnp.where(lowu, zero, u)], axis=0)
            r0, r1 = rows[base + s], rows[base + 16 + s]
            c0, c1 = cols[base + s], cols[base + 16 + s]
            xc = jnp.where(low, x2c[c0], x2c[c1])
            xr = jnp.where(low, x2r[r0], x2r[r1])
            fo = lax.dot_general(xc, bd, (((1,), (1,)), ((), ())), preferred_element_type=jnp.float32)
            co = lax.dot_general(xr, bd, (((1,), (0,)), ((), ())), preferred_element_type=jnp.float32)
            q = s % copies
            f_acc[2 * q][r0] += fo
            f_acc[2 * q + 1][r1] += fo
            c_acc[2 * q][c0] += co
            c_acc[2 * q + 1][c1] += co

    fetch(0).wait()
    relayout(0, stages[0])

    @pl.loop(0, chunks // 2)
    def _(h):
        for e in range(2):
            k = 2 * h + e
            nxt = jnp.minimum(k + 1, chunks - 1)
            @pl.when(k + 1 < chunks)
            def _():
                fetch(k + 1).wait()
            relayout(nxt, stages[1 - e])
            compute(k * 32, stages[e])

    @pl.loop(0, 16)
    def _(b):
        low = lane_low((16, 128))
        for acc, out in ((f_acc, f_out), (c_acc, c_out)):
            for t in range(4):
                parts = []
                for u in range(2):
                    r = b * 8 + 2 * t + u
                    g0 = acc[0][r]
                    g1 = acc[1][r]
                    for q in range(1, copies):
                        g0 = g0 + acc[2 * q][r]
                        g1 = g1 + acc[2 * q + 1][r]
                    parts.append(g0[:, :64] + g1[:, 64:])
                out[b, :, t * 128:(t + 1) * 128] = jnp.concatenate(parts, axis=1)

def local_products(rows, cols, count, row_set, col_set, tiles, copies=1):
    out = jax.ShapeDtypeStruct((16, 16, 512), jnp.float32)
    smem = pl.BlockSpec(memory_space=pltpu.SMEM)
    vmem = pl.BlockSpec(memory_space=pltpu.VMEM)
    return pl.pallas_call(
        functools.partial(local_kernel, copies),
        out_shape=(out, out),
        in_specs=[smem, smem, smem, vmem, vmem, pl.BlockSpec(memory_space=pl.ANY)],
        out_specs=(vmem, vmem),
        scratch_shapes=[
            pltpu.VMEM((1024, 4096), jnp.bfloat16),
            pltpu.SemaphoreType.DMA((32,)),
            pltpu.VMEM((128, 16, 128), jnp.bfloat16),
            pltpu.VMEM((128, 16, 128), jnp.bfloat16),
            pltpu.VMEM((1024, 128), jnp.float32),
            pltpu.VMEM((1024, 128), jnp.float32),
        ] + [pltpu.VMEM((128, 16, 128), jnp.float32)] * (4 * copies),
        compiler_params=pltpu.CompilerParams(vmem_limit_bytes=60 << 20),
        name="local_products",
    )(rows, cols, count, row_set, col_set, tiles)


def on_device(vectors, tiles, tile_rows, tile_cols, tile_counts):
    row_set, col_set = gather(vectors)
    f, c = local_products(
        tile_rows.reshape(-1), tile_cols.reshape(-1), tile_counts.reshape(-1),
        row_set, col_set, tiles.reshape(tiles.shape[2:]))
    return scatter(f, c)


def solution(mesh):
    return jax.shard_map(
        on_device,
        mesh=mesh,
        in_specs=(
            P(None, ("row", "col")),
            P("row", "col", None, None),
            P("row", "col", None),
            P("row", "col", None),
            P("row", "col"),
        ),
        out_specs=P(None, ("row", "col")),
        check_vma=False,
    )
```

```python
import functools

import jax
import jax.numpy as jnp
from jax import lax
from jax.experimental import pallas as pl
from jax.experimental.pallas import tpu as pltpu
from jax.sharding import PartitionSpec as P

MESH = pl.DeviceIdType.MESH


class Place:
    def __init__(self):
        self.a, self.b = lax.axis_index("row"), lax.axis_index("col")
        self.y, self.h, self.k = self.a // 4, (self.a // 2) % 2, self.a % 2
        self.x, self.z = self.b // 4, self.b % 4

    def row(self, dy=0, dh=0, dk=0):
        return ((self.y + dy) % 4) * 4 + ((self.h + dh) % 2) * 2 + (self.k + dk) % 2

    def col(self, dx=0, dz=0):
        return ((self.x + dx) % 4) * 4 + (self.z + dz) % 4

    def meet(self):
        peers = [(self.row(dh=1), self.b), (self.row(dk=1), self.b)]
        peers += [(self.row(dy=d), self.b) for d in (1, 2, 3)]
        peers += [(self.a, self.col(dx=d)) for d in (1, 2, 3)]
        peers += [(self.a, self.col(dz=d)) for d in (1, 2, 3)]
        barrier = pltpu.get_barrier_semaphore()
        for peer in peers:
            pl.semaphore_signal(barrier, inc=1, device_id=peer, device_id_type=MESH)
        pl.semaphore_wait(barrier, len(peers))


class Sends:
    def __init__(self, sems):
        self.sems, self.started = sems, []

    def go(self, src, dst, recv_sem, device):
        copy = pltpu.make_async_remote_copy(
            src_ref=src, dst_ref=dst, send_sem=self.sems.at[len(self.started)],
            recv_sem=recv_sem, device_id=device, device_id_type=MESH)
        copy.start()
        self.started.append(copy)

    def arrived(self, dst, recv_sem, device):
        pltpu.make_async_remote_copy(
            src_ref=dst, dst_ref=dst, send_sem=self.sems.at[0],
            recv_sem=recv_sem, device_id=device, device_id_type=MESH).wait_recv()

    def finish(self):
        for copy in self.started:
            copy.wait_send()


def gather_kernel(vec, row_set, col_set, send_sems, row_sems, col_sems):
    at = Place()
    a, b = at.a, at.b
    sends = Sends(send_sems)
    at.meet()
    mine_r, mine_c = row_set.at[b], col_set.at[a]
    sends.go(vec, mine_c, col_sems.at[a], (at.row(dh=1), b))
    for d in (2, 1, 3):
        sends.go(vec, mine_r, row_sems.at[b], (a, at.col(dz=d)))
    for d in (2, 1, 3):
        sends.go(vec, mine_c, col_sems.at[a], (at.row(dy=d), b))
    for d in (2, 1, 3):
        sends.go(vec, mine_r, row_sems.at[b], (a, at.col(dx=d)))
    sends.go(vec, mine_c, col_sems.at[a], (at.row(dk=1), b))
    row_set[b] = vec[...]
    col_set[a] = vec[...]

    def got_r(j):
        sends.arrived(row_set.at[j], row_sems.at[j], (a, b))

    def got_c(j):
        sends.arrived(col_set.at[j], col_sems.at[j], (a, b))

    for d in (1, 3, 2):
        j = at.col(dz=d)
        got_r(j)
        for e in (2, 1, 3):
            sends.go(row_set.at[j], row_set.at[j], row_sems.at[j], (a, at.col(dx=e)))
    j = at.row(dh=1)
    got_c(j)
    for e in (2, 1, 3):
        sends.go(col_set.at[j], col_set.at[j], col_sems.at[j], (at.row(dy=e), b))
    sends.go(col_set.at[j], col_set.at[j], col_sems.at[j], (at.row(dk=1), b))
    for dh in (0, 1):
        for d in (1, 3, 2):
            j = at.row(dy=d, dh=dh)
            got_c(j)
            sends.go(col_set.at[j], col_set.at[j], col_sems.at[j], (at.row(dk=1), b))
    for dh in (0, 1):
        for d in (0, 1, 2, 3):
            got_c(at.row(dy=d, dh=dh, dk=1))
    for d in (1, 3, 2):
        for e in (0, 1, 3, 2):
            got_r(at.col(dx=d, dz=e))
    sends.finish()


def gather(vectors):
    whole = jax.ShapeDtypeStruct((16,) + vectors.shape, vectors.dtype)
    vmem = pl.BlockSpec(memory_space=pltpu.VMEM)
    return pl.pallas_call(
        gather_kernel,
        out_shape=(whole, whole),
        in_specs=[vmem],
        out_specs=(vmem, vmem),
        scratch_shapes=[
            pltpu.SemaphoreType.DMA((30,)),
            pltpu.SemaphoreType.DMA((16,)),
            pltpu.SemaphoreType.DMA((16,)),
        ],
        compiler_params=pltpu.CompilerParams(
            collective_id=0, has_side_effects=True, vmem_limit_bytes=8 << 20),
        cost_estimate=pl.CostEstimate(flops=10**10, bytes_accessed=2**22, transcendentals=0),
        name="gather",
    )(vectors)


def scatter_kernel(f, c, out, fx, fs, fz, cc, cs, cy, ch, send_sems, fx_sems, fz_sems, cc_sems, cy_sems, ch_sem):
    at = Place()
    a, b = at.a, at.b
    sends = Sends(send_sems)
    at.meet()
    far = (2, 1, 3)
    for dy in (2, 1, 3, 0):
        for dh in (1, 0):
            n = dy * 2 + dh
            sends.go(c.at[at.row(dy=dy, dh=dh, dk=1)], cc.at[n], cc_sems.at[n], (at.row(dk=1), b))
    for dz in (2, 1, 3, 0):
        for dx in far:
            n = dz * 3 + dx - 1
            sends.go(f.at[at.col(dx=dx, dz=dz)], fx.at[n], fx_sems.at[n], (a, at.col(dx=dx)))

    def sum_core(dy, dh):
        n = dy * 2 + dh
        sends.arrived(cc.at[n], cc_sems.at[n], (a, b))
        cs[n] = c[at.row(dy=dy, dh=dh)] + cc[n]

    def sum_x(dz):
        for dx in far:
            n = dz * 3 + dx - 1
            sends.arrived(fx.at[n], fx_sems.at[n], (a, b))
        fs[dz] = (f[at.col(dz=dz)] + fx[dz * 3]) + (fx[dz * 3 + 1] + fx[dz * 3 + 2])

    def sum_y(dh):
        for dy in far:
            n = (dy - 1) * 2 + dh
            sends.arrived(cy.at[n], cy_sems.at[n], (a, b))
        cs[dh] = (cs[dh] + cy[dh]) + (cy[2 + dh] + cy[4 + dh])

    for dy in far:
        for dh in (1, 0):
            sum_core(dy, dh)
            n = (dy - 1) * 2 + dh
            sends.go(cs.at[dy * 2 + dh], cy.at[n], cy_sems.at[n], (at.row(dy=dy), b))
    sum_core(0, 1)
    sum_core(0, 0)
    for dz in far:
        sum_x(dz)
        sends.go(fs.at[dz], fz.at[dz - 1], fz_sems.at[dz - 1], (a, at.col(dz=dz)))
        if dz == 2:
            sum_y(1)
            sends.go(cs.at[1], ch, ch_sem, (at.row(dh=1), b))
    sum_y(0)
    sum_x(0)
    sends.arrived(ch, ch_sem, (a, b))
    total = fs[0] + (cs[0] + ch[...])
    for dz in (1, 3, 2):
        sends.arrived(fz.at[dz - 1], fz_sems.at[dz - 1], (a, b))
    out[...] = total + (fz[0] + (fz[1] + fz[2]))
    sends.finish()


def scatter(f, c):
    block = f.shape[1:]
    vmem = pl.BlockSpec(memory_space=pltpu.VMEM)

    def room(n):
        return pltpu.VMEM((n,) + block, jnp.float32)

    return pl.pallas_call(
        scatter_kernel,
        out_shape=jax.ShapeDtypeStruct(block, jnp.float32),
        in_specs=[vmem, vmem],
        out_specs=vmem,
        scratch_shapes=[
            room(12), room(4), room(3), room(8), room(8), room(6), pltpu.VMEM(block, jnp.float32),
            pltpu.SemaphoreType.DMA((30,)),
            pltpu.SemaphoreType.DMA((12,)),
            pltpu.SemaphoreType.DMA((3,)),
            pltpu.SemaphoreType.DMA((8,)),
            pltpu.SemaphoreType.DMA((6,)),
            pltpu.SemaphoreType.DMA,
        ],
        compiler_params=pltpu.CompilerParams(
            collective_id=1, has_side_effects=True, vmem_limit_bytes=8 << 20),
        name="scatter",
    )(f, c)


PITCH = 17
UNROLL = 4


def lane_low(shape):
    return lax.broadcasted_iota(jnp.int32, shape, 1) < 64

def halves(v):
    lo, hi = v[:, :64], v[:, 64:]
    return jnp.concatenate([lo, lo], axis=1), jnp.concatenate([hi, hi], axis=1)

def local_kernel(copies, rows, cols, count, row_set, col_set, tiles, f_out, c_out, *scratch):
    tbuf, tsem, x2r, x2c = scratch[:4]
    stages = scratch[4:6]
    f_acc = scratch[6:6 + 2 * copies]
    c_acc = scratch[6 + 2 * copies:6 + 4 * copies]
    chunks = count[0] // 32

    def fetch(k):
        at = pl.ds(pl.multiple_of(k * 32, 32), 32)
        return pltpu.make_async_copy(tiles.at[at, :], tbuf.at[at, :], tsem.at[k])

    @pl.loop(0, chunks)
    def _(k):
        fetch(k).start()

    @pl.loop(0, 128, unroll=8)
    def _(r):
        for acc in f_acc + c_acc:
            acc[r] = jnp.zeros((16, 128), jnp.float32)

    @pl.loop(0, 16, unroll=2)
    def _(b):
        for src, dst in ((row_set, x2r), (col_set, x2c)):
            for t in range(4):
                lo, hi = halves(src[b, :, t * 128:(t + 1) * 128])
                dst[b * 8 + 2 * t] = lo
                dst[b * 8 + 2 * t + 1] = hi

    def relayout(k, stage, p):
        at = pl.multiple_of(k * 32, 32)
        v0 = tbuf[pl.ds(at, 16), p * 128:(p + 1) * 128]
        v1 = tbuf[pl.ds(pl.multiple_of(at + 16, 16), 16), p * 128:(p + 1) * 128]
        even = jnp.concatenate([v0[:, :64], v1[:, :64]], axis=1)
        odd = jnp.concatenate([v0[:, 64:], v1[:, 64:]], axis=1)
        stage[pl.ds(PITCH * 2 * p, 16), :] = even.astype(jnp.float32)
        stage[pl.ds(PITCH * (2 * p + 1), 16), :] = odd.astype(jnp.float32)

    low = lane_low((16, 128))
    lowu = lane_low((64, 128))
    nothing = jnp.zeros((16, 128), jnp.bfloat16)

    def blocks(stage, s):
        u = stage[pl.ds(s, 64, stride=PITCH), :].astype(jnp.bfloat16)
        zero = jnp.zeros_like(u)
        return jnp.concatenate([jnp.where(lowu, u, zero), jnp.where(lowu, zero, u)], axis=0)

    def pick(table, i, j):
        return jnp.where(low, table[i], table[j])

    def two_pairs(base, stage, s):
        bd = [blocks(stage, s), blocks(stage, s + 1)]
        r = [(rows[base + s + e], rows[base + 16 + s + e]) for e in (0, 1)]
        c = [(cols[base + s + e], cols[base + 16 + s + e]) for e in (0, 1)]

        def spread(x):
            return jnp.concatenate([jnp.concatenate([x[0], nothing], axis=1),
                                    jnp.concatenate([nothing, x[1]], axis=1)], axis=0)

        xc = spread([pick(x2c, *c[e]) for e in (0, 1)])
        xr = spread([pick(x2r, *r[e]) for e in (0, 1)])
        fo = lax.dot_general(xc, jnp.concatenate(bd, axis=1), (((1,), (1,)), ((), ())),
                             preferred_element_type=jnp.float32)
        co = lax.dot_general(xr, jnp.concatenate(bd, axis=0), (((1,), (0,)), ((), ())),
                             preferred_element_type=jnp.float32)
        for e in (0, 1):
            q = e % copies
            f_acc[2 * q][r[e][0]] += fo[16 * e:16 * e + 16]
            f_acc[2 * q + 1][r[e][1]] += fo[16 * e:16 * e + 16]
            c_acc[2 * q][c[e][0]] += co[16 * e:16 * e + 16]
            c_acc[2 * q + 1][c[e][1]] += co[16 * e:16 * e + 16]

    fetch(0).wait()
    for p in range(32):
        relayout(0, stages[0], p)

    @pl.loop(0, chunks // UNROLL)
    def _(h):
        first = h * UNROLL
        for e in range(1, UNROLL):
            fetch(first + e).wait()

        @pl.when(first + UNROLL < chunks)
        def _():
            fetch(first + UNROLL).wait()

        for e in range(UNROLL):
            k = first + e
            nxt = k + 1 if e < UNROLL - 1 else jnp.minimum(k + 1, chunks - 1)
            for s in range(0, 16, 2):
                two_pairs(k * 32, stages[e % 2], s)
                for p in range(2 * s, 2 * s + 4):
                    relayout(nxt, stages[1 - e % 2], p)

    @pl.loop(0, 16, unroll=2)
    def _(b):
        low = lane_low((16, 128))
        for acc, out in ((f_acc, f_out), (c_acc, c_out)):
            for t in range(4):
                parts = []
                for u in range(2):
                    r = b * 8 + 2 * t + u
                    g0 = acc[0][r]
                    g1 = acc[1][r]
                    for q in range(1, copies):
                        g0 = g0 + acc[2 * q][r]
                        g1 = g1 + acc[2 * q + 1][r]
                    parts.append(g0[:, :64] + g1[:, 64:])
                out[b, :, t * 128:(t + 1) * 128] = jnp.concatenate(parts, axis=1)

def local_products(rows, cols, count, row_set, col_set, tiles, copies=1):
    out = jax.ShapeDtypeStruct((16, 16, 512), jnp.float32)
    smem = pl.BlockSpec(memory_space=pltpu.SMEM)
    vmem = pl.BlockSpec(memory_space=pltpu.VMEM)
    return pl.pallas_call(
        functools.partial(local_kernel, copies),
        out_shape=(out, out),
        in_specs=[smem, smem, smem, vmem, vmem, pl.BlockSpec(memory_space=pl.ANY)],
        out_specs=(vmem, vmem),
        scratch_shapes=[
            pltpu.VMEM((1024, 4096), jnp.bfloat16),
            pltpu.SemaphoreType.DMA((32,)),
            pltpu.VMEM((128, 16, 128), jnp.bfloat16),
            pltpu.VMEM((128, 16, 128), jnp.bfloat16),
            pltpu.VMEM((64 * PITCH, 128), jnp.float32),
            pltpu.VMEM((64 * PITCH, 128), jnp.float32),
        ] + [pltpu.VMEM((128, 16, 128), jnp.float32)] * (4 * copies),
        compiler_params=pltpu.CompilerParams(vmem_limit_bytes=24 << 20),
        name="local_products",
    )(rows, cols, count, row_set, col_set, tiles)


def on_device(vectors, tiles, tile_rows, tile_cols, tile_counts):
    row_set, col_set = gather(vectors)
    f, c = local_products(
        tile_rows.reshape(-1), tile_cols.reshape(-1), tile_counts.reshape(-1),
        row_set, col_set, tiles.reshape(tiles.shape[2:]))
    return scatter(f, c)


def solution(mesh):
    return jax.shard_map(
        on_device,
        mesh=mesh,
        in_specs=(
            P(None, ("row", "col")),
            P("row", "col", None, None),
            P("row", "col", None),
            P("row", "col", None),
            P("row", "col"),
        ),
        out_specs=P(None, ("row", "col")),
        check_vma=False,
    )
```

```python
import functools

import jax
import jax.numpy as jnp
from jax import lax
from jax.experimental import pallas as pl
from jax.experimental.pallas import tpu as pltpu
from jax.sharding import PartitionSpec as P

MESH = pl.DeviceIdType.MESH


class Place:
    def __init__(self):
        self.a, self.b = lax.axis_index("row"), lax.axis_index("col")
        self.y, self.h, self.k = self.a // 4, (self.a // 2) % 2, self.a % 2
        self.x, self.z = self.b // 4, self.b % 4

    def row(self, dy=0, dh=0, dk=0):
        return ((self.y + dy) % 4) * 4 + ((self.h + dh) % 2) * 2 + (self.k + dk) % 2

    def col(self, dx=0, dz=0):
        return ((self.x + dx) % 4) * 4 + (self.z + dz) % 4

    def greet(self):
        peers = [(self.row(dh=1), self.b), (self.row(dk=1), self.b)]
        peers += [(self.row(dy=d), self.b) for d in (1, 2, 3)]
        peers += [(self.a, self.col(dx=d)) for d in (1, 2, 3)]
        peers += [(self.a, self.col(dz=d)) for d in (1, 2, 3)]
        barrier = pltpu.get_barrier_semaphore()
        for peer in peers:
            pl.semaphore_signal(barrier, inc=1, device_id=peer, device_id_type=MESH)
        return lambda: pl.semaphore_wait(barrier, len(peers))


class Sends:
    def __init__(self, sems):
        self.sems, self.started = sems, []

    def go(self, src, dst, recv_sem, device):
        copy = pltpu.make_async_remote_copy(
            src_ref=src, dst_ref=dst, send_sem=self.sems.at[len(self.started)],
            recv_sem=recv_sem, device_id=device, device_id_type=MESH)
        copy.start()
        self.started.append(copy)

    def arrived(self, dst, recv_sem, device):
        pltpu.make_async_remote_copy(
            src_ref=dst, dst_ref=dst, send_sem=self.sems.at[0],
            recv_sem=recv_sem, device_id=device, device_id_type=MESH).wait_recv()

    def finish(self):
        for copy in self.started:
            copy.wait_send()


def halves(v):
    lo, hi = v[:, :64], v[:, 64:]
    return jnp.concatenate([lo, lo], axis=1), jnp.concatenate([hi, hi], axis=1)


def gather_kernel(vec, x2r, x2c, f_low, f_high, c_low, c_high, row_set, col_set, send_sems, row_sems, col_sems):
    at = Place()
    a, b = at.a, at.b
    sends = Sends(send_sems)
    meet = at.greet()

    @pl.loop(0, 128, unroll=8)
    def _(r):
        for acc in (f_low, f_high, c_low, c_high):
            acc[r] = jnp.zeros((16, 128), jnp.float32)

    meet()
    mine_r, mine_c = row_set.at[b], col_set.at[a]
    sends.go(vec, mine_c, col_sems.at[a], (at.row(dh=1), b))
    for d in (2, 1, 3):
        sends.go(vec, mine_r, row_sems.at[b], (a, at.col(dz=d)))
    for d in (2, 1, 3):
        sends.go(vec, mine_c, col_sems.at[a], (at.row(dy=d), b))
    for d in (2, 1, 3):
        sends.go(vec, mine_r, row_sems.at[b], (a, at.col(dx=d)))
    sends.go(vec, mine_c, col_sems.at[a], (at.row(dk=1), b))
    row_set[b] = vec[...]
    col_set[a] = vec[...]

    def widen(src, dst, j):
        for t in range(4):
            lo, hi = halves(src[j, :, t * 128:(t + 1) * 128])
            dst[j * 8 + 2 * t] = lo
            dst[j * 8 + 2 * t + 1] = hi

    widen(row_set, x2r, b)
    widen(col_set, x2c, a)

    def got_r(j):
        sends.arrived(row_set.at[j], row_sems.at[j], (a, b))

    def got_c(j):
        sends.arrived(col_set.at[j], col_sems.at[j], (a, b))

    for d in (1, 3, 2):
        j = at.col(dz=d)
        got_r(j)
        for e in (2, 1, 3):
            sends.go(row_set.at[j], row_set.at[j], row_sems.at[j], (a, at.col(dx=e)))
    j = at.row(dh=1)
    got_c(j)
    for e in (2, 1, 3):
        sends.go(col_set.at[j], col_set.at[j], col_sems.at[j], (at.row(dy=e), b))
    sends.go(col_set.at[j], col_set.at[j], col_sems.at[j], (at.row(dk=1), b))
    for dh in (0, 1):
        for d in (1, 3, 2):
            j = at.row(dy=d, dh=dh)
            got_c(j)
            sends.go(col_set.at[j], col_set.at[j], col_sems.at[j], (at.row(dk=1), b))
    for d in (1, 2, 3):
        widen(row_set, x2r, at.col(dz=d))
        widen(col_set, x2c, at.row(dy=d))
    for d in (0, 1, 2, 3):
        widen(col_set, x2c, at.row(dy=d, dh=1))
    for dh in (0, 1):
        for d in (0, 1, 2, 3):
            j = at.row(dy=d, dh=dh, dk=1)
            got_c(j)
            widen(col_set, x2c, j)
    for d in (1, 3, 2):
        for e in (0, 1, 3, 2):
            j = at.col(dx=d, dz=e)
            got_r(j)
            widen(row_set, x2r, j)
    sends.finish()


def gather(vectors):
    whole = pltpu.VMEM((16,) + vectors.shape, vectors.dtype)
    table = jax.ShapeDtypeStruct((128, 16, 128), vectors.dtype)
    sums = jax.ShapeDtypeStruct((128, 16, 128), jnp.float32)
    vmem = pl.BlockSpec(memory_space=pltpu.VMEM)
    return pl.pallas_call(
        gather_kernel,
        out_shape=(table,) * 2 + (sums,) * 4,
        in_specs=[vmem],
        out_specs=(vmem,) * 6,
        scratch_shapes=[
            whole, whole,
            pltpu.SemaphoreType.DMA((30,)),
            pltpu.SemaphoreType.DMA((16,)),
            pltpu.SemaphoreType.DMA((16,)),
        ],
        compiler_params=pltpu.CompilerParams(
            collective_id=0, has_side_effects=True, vmem_limit_bytes=8 << 20),
        cost_estimate=pl.CostEstimate(flops=10**10, bytes_accessed=2**22, transcendentals=0),
        name="gather",
    )(vectors)


def scatter_kernel(f_low, f_high, c_low, c_high, out, f, c, fx, fs, fz, cc, cs, cy, ch,
                   send_sems, fx_sems, fz_sems, cc_sems, cy_sems, ch_sem):
    at = Place()
    a, b = at.a, at.b
    sends = Sends(send_sems)
    meet = at.greet()
    far = (2, 1, 3)

    def emit(low, high, whole, j):
        for t in range(4):
            parts = [low[j * 8 + 2 * t + u, :, :64] + high[j * 8 + 2 * t + u, :, 64:] for u in (0, 1)]
            whole[j, :, t * 128:(t + 1) * 128] = jnp.concatenate(parts, axis=1)

    def emit_f(j):
        emit(f_low, f_high, f, j)

    def emit_c(j):
        emit(c_low, c_high, c, j)

    def send_f(dz):
        for dx in far:
            n = dz * 3 + dx - 1
            j = at.col(dx=dx, dz=dz)
            if dz != 2:
                emit_f(j)
            sends.go(f.at[j], fx.at[n], fx_sems.at[n], (a, at.col(dx=dx)))

    def send_c(dy):
        for dh in (1, 0):
            n = dy * 2 + dh
            j = at.row(dy=dy, dh=dh, dk=1)
            if dy != 2:
                emit_c(j)
            sends.go(c.at[j], cc.at[n], cc_sems.at[n], (at.row(dk=1), b))

    for dx in far:
        emit_f(at.col(dx=dx, dz=2))
    for dh in (1, 0):
        emit_c(at.row(dy=2, dh=dh, dk=1))
    meet()
    for d in (2, 1, 3, 0):
        send_f(d)
        send_c(d)
    for d in (2, 1, 3, 0):
        emit_f(at.col(dz=d))
        for dh in (1, 0):
            emit_c(at.row(dy=d, dh=dh))

    def sum_core(dy, dh):
        n = dy * 2 + dh
        sends.arrived(cc.at[n], cc_sems.at[n], (a, b))
        cs[n] = c[at.row(dy=dy, dh=dh)] + cc[n]

    def sum_x(dz):
        for dx in far:
            n = dz * 3 + dx - 1
            sends.arrived(fx.at[n], fx_sems.at[n], (a, b))
        fs[dz] = (f[at.col(dz=dz)] + fx[dz * 3]) + (fx[dz * 3 + 1] + fx[dz * 3 + 2])

    def sum_y(dh):
        for dy in far:
            n = (dy - 1) * 2 + dh
            sends.arrived(cy.at[n], cy_sems.at[n], (a, b))
        cs[dh] = (cs[dh] + cy[dh]) + (cy[2 + dh] + cy[4 + dh])

    for dy in far:
        for dh in (1, 0):
            sum_core(dy, dh)
            n = (dy - 1) * 2 + dh
            sends.go(cs.at[dy * 2 + dh], cy.at[n], cy_sems.at[n], (at.row(dy=dy), b))
    sum_core(0, 1)
    sum_core(0, 0)
    for dz in far:
        sum_x(dz)
        sends.go(fs.at[dz], fz.at[dz - 1], fz_sems.at[dz - 1], (a, at.col(dz=dz)))
        if dz == 2:
            sum_y(1)
            sends.go(cs.at[1], ch, ch_sem, (at.row(dh=1), b))
    sum_y(0)
    sum_x(0)
    sends.arrived(ch, ch_sem, (a, b))
    total = fs[0] + (cs[0] + ch[...])
    for dz in (1, 3, 2):
        sends.arrived(fz.at[dz - 1], fz_sems.at[dz - 1], (a, b))
    out[...] = total + (fz[0] + (fz[1] + fz[2]))
    sends.finish()


def scatter(block, sums):
    vmem = pl.BlockSpec(memory_space=pltpu.VMEM)

    def room(n):
        return pltpu.VMEM((n,) + block, jnp.float32)

    return pl.pallas_call(
        scatter_kernel,
        out_shape=jax.ShapeDtypeStruct(block, jnp.float32),
        in_specs=[vmem] * 4,
        out_specs=vmem,
        scratch_shapes=[
            room(16), room(16), room(12), room(4), room(3), room(8), room(8), room(6), pltpu.VMEM(block, jnp.float32),
            pltpu.SemaphoreType.DMA((30,)),
            pltpu.SemaphoreType.DMA((12,)),
            pltpu.SemaphoreType.DMA((3,)),
            pltpu.SemaphoreType.DMA((8,)),
            pltpu.SemaphoreType.DMA((6,)),
            pltpu.SemaphoreType.DMA,
        ],
        compiler_params=pltpu.CompilerParams(
            collective_id=1, has_side_effects=True, vmem_limit_bytes=8 << 20),
        name="scatter",
    )(*sums)


PITCH = 17
UNROLL = 4


def lane_low(shape):
    return lax.broadcasted_iota(jnp.int32, shape, 1) < 64


def local_kernel(rows, cols, count, x2r, x2c, tiles, f0, f1, c0, c1, f_low, f_high, c_low, c_high, *stages):
    f_acc, c_acc = (f_low, f_high), (c_low, c_high)
    chunks = count[0] // 32

    def relayout(k, stage, p):
        at = pl.multiple_of(k * 32, 32)
        v0 = tiles[pl.ds(at, 16), p * 128:(p + 1) * 128]
        v1 = tiles[pl.ds(pl.multiple_of(at + 16, 16), 16), p * 128:(p + 1) * 128]
        even = jnp.concatenate([v0[:, :64], v1[:, :64]], axis=1)
        odd = jnp.concatenate([v0[:, 64:], v1[:, 64:]], axis=1)
        stage[pl.ds(PITCH * 2 * p, 16), :] = even.astype(jnp.float32)
        stage[pl.ds(PITCH * (2 * p + 1), 16), :] = odd.astype(jnp.float32)

    low = lane_low((16, 128))
    lowu = lane_low((64, 128))
    nothing = jnp.zeros((16, 128), jnp.bfloat16)

    def blocks(stage, s):
        u = stage[pl.ds(s, 64, stride=PITCH), :].astype(jnp.bfloat16)
        zero = jnp.zeros_like(u)
        return jnp.concatenate([jnp.where(lowu, u, zero), jnp.where(lowu, zero, u)], axis=0)

    def pick(table, i, j):
        return jnp.where(low, table[i], table[j])

    def two_pairs(base, stage, s):
        bd = [blocks(stage, s), blocks(stage, s + 1)]
        r = [(rows[base + s + e], rows[base + 16 + s + e]) for e in (0, 1)]
        c = [(cols[base + s + e], cols[base + 16 + s + e]) for e in (0, 1)]

        def spread(x):
            return jnp.concatenate([jnp.concatenate([x[0], nothing], axis=1),
                                    jnp.concatenate([nothing, x[1]], axis=1)], axis=0)

        xc = spread([pick(x2c, *c[e]) for e in (0, 1)])
        xr = spread([pick(x2r, *r[e]) for e in (0, 1)])
        fo = lax.dot_general(xc, jnp.concatenate(bd, axis=1), (((1,), (1,)), ((), ())),
                             preferred_element_type=jnp.float32)
        co = lax.dot_general(xr, jnp.concatenate(bd, axis=0), (((1,), (0,)), ((), ())),
                             preferred_element_type=jnp.float32)
        for e in (0, 1):
            f_acc[0][r[e][0]] += fo[16 * e:16 * e + 16]
            f_acc[1][r[e][1]] += fo[16 * e:16 * e + 16]
            c_acc[0][c[e][0]] += co[16 * e:16 * e + 16]
            c_acc[1][c[e][1]] += co[16 * e:16 * e + 16]

    for p in range(32):
        relayout(0, stages[0], p)

    @pl.loop(0, chunks // UNROLL)
    def _(h):
        first = h * UNROLL
        for e in range(UNROLL):
            k = first + e
            nxt = k + 1 if e < UNROLL - 1 else jnp.minimum(k + 1, chunks - 1)
            for s in range(0, 16, 2):
                two_pairs(k * 32, stages[e % 2], s)
                for p in range(2 * s, 2 * s + 4):
                    relayout(nxt, stages[1 - e % 2], p)


def local_products(rows, cols, count, x2r, x2c, tiles, sums):
    smem = pl.BlockSpec(memory_space=pltpu.SMEM)
    vmem = pl.BlockSpec(memory_space=pltpu.VMEM)
    return pl.pallas_call(
        local_kernel,
        out_shape=tuple(jax.ShapeDtypeStruct(v.shape, v.dtype) for v in sums),
        in_specs=[smem] * 3 + [vmem] * 7,
        out_specs=(vmem,) * 4,
        input_output_aliases={6: 0, 7: 1, 8: 2, 9: 3},
        scratch_shapes=[pltpu.VMEM((64 * PITCH, 128), jnp.float32)] * 2,
        compiler_params=pltpu.CompilerParams(vmem_limit_bytes=24 << 20),
        name="local_products",
    )(rows, cols, count, x2r, x2c, tiles, *sums)


def on_device(vectors, tiles, tile_rows, tile_cols, tile_counts):
    x2r, x2c, *sums = gather(vectors)
    sums = local_products(
        tile_rows.reshape(-1), tile_cols.reshape(-1), tile_counts.reshape(-1),
        x2r, x2c, tiles.reshape(tiles.shape[2:]), sums)
    return scatter(vectors.shape, sums)


def solution(mesh):
    return jax.shard_map(
        on_device,
        mesh=mesh,
        in_specs=(
            P(None, ("row", "col")),
            P("row", "col", None, None),
            P("row", "col", None),
            P("row", "col", None),
            P("row", "col"),
        ),
        out_specs=P(None, ("row", "col")),
        check_vma=False,
    )
```

```python
import functools

import jax
import jax.numpy as jnp
from jax import lax
from jax.experimental import pallas as pl
from jax.experimental.pallas import tpu as pltpu
from jax.sharding import PartitionSpec as P

MESH = pl.DeviceIdType.MESH


class Place:
    def __init__(self):
        self.a, self.b = lax.axis_index("row"), lax.axis_index("col")
        self.y, self.h, self.k = self.a // 4, (self.a // 2) % 2, self.a % 2
        self.x, self.z = self.b // 4, self.b % 4

    def row(self, dy=0, dh=0, dk=0):
        return ((self.y + dy) % 4) * 4 + ((self.h + dh) % 2) * 2 + (self.k + dk) % 2

    def col(self, dx=0, dz=0):
        return ((self.x + dx) % 4) * 4 + (self.z + dz) % 4

    def greet(self):
        peers = [(self.row(dh=1), self.b), (self.row(dk=1), self.b)]
        peers += [(self.row(dy=d), self.b) for d in (1, 2, 3)]
        peers += [(self.a, self.col(dx=d)) for d in (1, 2, 3)]
        peers += [(self.a, self.col(dz=d)) for d in (1, 2, 3)]
        barrier = pltpu.get_barrier_semaphore()
        for peer in peers:
            pl.semaphore_signal(barrier, inc=1, device_id=peer, device_id_type=MESH)
        return lambda: pl.semaphore_wait(barrier, len(peers))


class Sends:
    def __init__(self, sems):
        self.sems, self.started = sems, []

    def go(self, src, dst, recv_sem, device):
        copy = pltpu.make_async_remote_copy(
            src_ref=src, dst_ref=dst, send_sem=self.sems.at[len(self.started)],
            recv_sem=recv_sem, device_id=device, device_id_type=MESH)
        copy.start()
        self.started.append(copy)

    def arrived(self, dst, recv_sem, device):
        pltpu.make_async_remote_copy(
            src_ref=dst, dst_ref=dst, send_sem=self.sems.at[0],
            recv_sem=recv_sem, device_id=device, device_id_type=MESH).wait_recv()

    def finish(self):
        for copy in self.started:
            copy.wait_send()


def halves(v):
    lo, hi = v[:, :64], v[:, 64:]
    return jnp.concatenate([lo, lo], axis=1), jnp.concatenate([hi, hi], axis=1)


def gather_kernel(vec, x2r, x2c, f_low, f_high, c_low, c_high, row_set, col_set, own_sems, send_sems, row_sems, col_sems):
    at = Place()
    a, b = at.a, at.b
    sends = Sends(send_sems)
    meet = at.greet()
    own = [pltpu.make_async_copy(vec, row_set.at[b], own_sems.at[0]),
           pltpu.make_async_copy(vec, col_set.at[a], own_sems.at[1])]
    for copy in own:
        copy.start()

    @pl.loop(0, 128, unroll=8)
    def _(r):
        for acc in (f_low, f_high, c_low, c_high):
            acc[r] = jnp.zeros((16, 128), jnp.float32)

    for copy in own:
        copy.wait()
    meet()
    mine_r, mine_c = row_set.at[b], col_set.at[a]
    sends.go(mine_c, mine_c, col_sems.at[a], (at.row(dh=1), b))
    for d in (2, 1, 3):
        sends.go(mine_r, mine_r, row_sems.at[b], (a, at.col(dz=d)))
    for d in (2, 1, 3):
        sends.go(mine_c, mine_c, col_sems.at[a], (at.row(dy=d), b))
    for d in (2, 1, 3):
        sends.go(mine_r, mine_r, row_sems.at[b], (a, at.col(dx=d)))
    sends.go(mine_c, mine_c, col_sems.at[a], (at.row(dk=1), b))

    def widen(src, dst, j):
        for t in range(4):
            lo, hi = halves(src[j, :, t * 128:(t + 1) * 128])
            dst[j * 8 + 2 * t] = lo
            dst[j * 8 + 2 * t + 1] = hi

    widen(row_set, x2r, b)
    widen(col_set, x2c, a)

    def got_r(j):
        sends.arrived(row_set.at[j], row_sems.at[j], (a, b))

    def got_c(j):
        sends.arrived(col_set.at[j], col_sems.at[j], (a, b))

    for d in (1, 3, 2):
        j = at.col(dz=d)
        got_r(j)
        for e in (2, 1, 3):
            sends.go(row_set.at[j], row_set.at[j], row_sems.at[j], (a, at.col(dx=e)))
    j = at.row(dh=1)
    got_c(j)
    for e in (2, 1, 3):
        sends.go(col_set.at[j], col_set.at[j], col_sems.at[j], (at.row(dy=e), b))
    sends.go(col_set.at[j], col_set.at[j], col_sems.at[j], (at.row(dk=1), b))
    for dh in (0, 1):
        for d in (1, 3, 2):
            j = at.row(dy=d, dh=dh)
            got_c(j)
            sends.go(col_set.at[j], col_set.at[j], col_sems.at[j], (at.row(dk=1), b))
    for d in (1, 2, 3):
        widen(row_set, x2r, at.col(dz=d))
        widen(col_set, x2c, at.row(dy=d))
    for d in (0, 1, 2, 3):
        widen(col_set, x2c, at.row(dy=d, dh=1))
    for dh in (0, 1):
        for d in (0, 1, 2, 3):
            j = at.row(dy=d, dh=dh, dk=1)
            got_c(j)
            widen(col_set, x2c, j)
    for d in (1, 3, 2):
        for e in (0, 1, 3, 2):
            j = at.col(dx=d, dz=e)
            got_r(j)
            widen(row_set, x2r, j)
    sends.finish()


def gather(vectors):
    whole = pltpu.VMEM((16,) + vectors.shape, vectors.dtype)
    table = jax.ShapeDtypeStruct((128, 16, 128), vectors.dtype)
    sums = jax.ShapeDtypeStruct((128, 16, 128), jnp.float32)
    vmem = pl.BlockSpec(memory_space=pltpu.VMEM)
    return pl.pallas_call(
        gather_kernel,
        out_shape=(table,) * 2 + (sums,) * 4,
        in_specs=[pl.BlockSpec(memory_space=pltpu.HBM)],
        out_specs=(vmem,) * 6,
        scratch_shapes=[
            whole, whole,
            pltpu.SemaphoreType.DMA((2,)),
            pltpu.SemaphoreType.DMA((30,)),
            pltpu.SemaphoreType.DMA((16,)),
            pltpu.SemaphoreType.DMA((16,)),
        ],
        compiler_params=pltpu.CompilerParams(
            collective_id=0, has_side_effects=True, vmem_limit_bytes=8 << 20),
        cost_estimate=pl.CostEstimate(flops=10**10, bytes_accessed=2**22, transcendentals=0),
        name="gather",
    )(vectors)


def scatter_kernel(f_low, f_high, c_low, c_high, out, f, c, fx, fs, fz, cc, cs, cy, ch,
                   send_sems, fx_sems, fz_sems, cc_sems, cy_sems, ch_sem):
    at = Place()
    a, b = at.a, at.b
    sends = Sends(send_sems)
    meet = at.greet()
    far = (2, 1, 3)

    def emit(low, high, whole, j):
        for t in range(4):
            parts = [low[j * 8 + 2 * t + u, :, :64] + high[j * 8 + 2 * t + u, :, 64:] for u in (0, 1)]
            whole[j, :, t * 128:(t + 1) * 128] = jnp.concatenate(parts, axis=1)

    def emit_f(j):
        emit(f_low, f_high, f, j)

    def emit_c(j):
        emit(c_low, c_high, c, j)

    def send_f(dz):
        for dx in far:
            n = dz * 3 + dx - 1
            j = at.col(dx=dx, dz=dz)
            if dz != 2:
                emit_f(j)
            sends.go(f.at[j], fx.at[n], fx_sems.at[n], (a, at.col(dx=dx)))

    def send_c(dy):
        for dh in (1, 0):
            n = dy * 2 + dh
            j = at.row(dy=dy, dh=dh, dk=1)
            if dy != 2:
                emit_c(j)
            sends.go(c.at[j], cc.at[n], cc_sems.at[n], (at.row(dk=1), b))

    for dx in far:
        emit_f(at.col(dx=dx, dz=2))
    for dh in (1, 0):
        emit_c(at.row(dy=2, dh=dh, dk=1))
    meet()
    for d in (2, 1, 3, 0):
        send_f(d)
        send_c(d)
    for d in (2, 1, 3, 0):
        emit_f(at.col(dz=d))
        for dh in (1, 0):
            emit_c(at.row(dy=d, dh=dh))

    def sum_core(dy, dh):
        n = dy * 2 + dh
        sends.arrived(cc.at[n], cc_sems.at[n], (a, b))
        cs[n] = c[at.row(dy=dy, dh=dh)] + cc[n]

    def sum_x(dz):
        for dx in far:
            n = dz * 3 + dx - 1
            sends.arrived(fx.at[n], fx_sems.at[n], (a, b))
        fs[dz] = (f[at.col(dz=dz)] + fx[dz * 3]) + (fx[dz * 3 + 1] + fx[dz * 3 + 2])

    def sum_y(dh):
        for dy in far:
            n = (dy - 1) * 2 + dh
            sends.arrived(cy.at[n], cy_sems.at[n], (a, b))
        cs[dh] = (cs[dh] + cy[dh]) + (cy[2 + dh] + cy[4 + dh])

    for dy in far:
        for dh in (1, 0):
            sum_core(dy, dh)
            n = (dy - 1) * 2 + dh
            sends.go(cs.at[dy * 2 + dh], cy.at[n], cy_sems.at[n], (at.row(dy=dy), b))
    sum_core(0, 1)
    sum_core(0, 0)
    for dz in far:
        sum_x(dz)
        sends.go(fs.at[dz], fz.at[dz - 1], fz_sems.at[dz - 1], (a, at.col(dz=dz)))
        if dz == 2:
            sum_y(1)
            sends.go(cs.at[1], ch, ch_sem, (at.row(dh=1), b))
    sum_y(0)
    sum_x(0)
    sends.arrived(ch, ch_sem, (a, b))
    total = fs[0] + (cs[0] + ch[...])
    for dz in (1, 3, 2):
        sends.arrived(fz.at[dz - 1], fz_sems.at[dz - 1], (a, b))
    out[...] = total + (fz[0] + (fz[1] + fz[2]))
    sends.finish()


def scatter(block, sums):
    vmem = pl.BlockSpec(memory_space=pltpu.VMEM)

    def room(n):
        return pltpu.VMEM((n,) + block, jnp.float32)

    return pl.pallas_call(
        scatter_kernel,
        out_shape=jax.ShapeDtypeStruct(block, jnp.float32),
        in_specs=[vmem] * 4,
        out_specs=vmem,
        scratch_shapes=[
            room(16), room(16), room(12), room(4), room(3), room(8), room(8), room(6), pltpu.VMEM(block, jnp.float32),
            pltpu.SemaphoreType.DMA((30,)),
            pltpu.SemaphoreType.DMA((12,)),
            pltpu.SemaphoreType.DMA((3,)),
            pltpu.SemaphoreType.DMA((8,)),
            pltpu.SemaphoreType.DMA((6,)),
            pltpu.SemaphoreType.DMA,
        ],
        compiler_params=pltpu.CompilerParams(
            collective_id=1, has_side_effects=True, vmem_limit_bytes=8 << 20),
        name="scatter",
    )(*sums)


PITCH = 17
UNROLL = 4


def lane_low(shape):
    return lax.broadcasted_iota(jnp.int32, shape, 1) < 64


def local_kernel(rows, cols, count, x2r, x2c, tiles, f0, f1, c0, c1, f_low, f_high, c_low, c_high, *stages):
    f_acc, c_acc = (f_low, f_high), (c_low, c_high)
    chunks = count[0] // 32

    def relayout(k, stage, p):
        at = pl.multiple_of(k * 32, 32)
        v0 = tiles[pl.ds(at, 16), p * 128:(p + 1) * 128]
        v1 = tiles[pl.ds(pl.multiple_of(at + 16, 16), 16), p * 128:(p + 1) * 128]
        even = jnp.concatenate([v0[:, :64], v1[:, :64]], axis=1)
        odd = jnp.concatenate([v0[:, 64:], v1[:, 64:]], axis=1)
        stage[pl.ds(PITCH * 2 * p, 16), :] = even.astype(jnp.float32)
        stage[pl.ds(PITCH * (2 * p + 1), 16), :] = odd.astype(jnp.float32)

    low = lane_low((16, 128))
    lowu = lane_low((64, 128))
    nothing = jnp.zeros((16, 128), jnp.bfloat16)

    def blocks(stage, s):
        u = stage[pl.ds(s, 64, stride=PITCH), :].astype(jnp.bfloat16)
        zero = jnp.zeros_like(u)
        return jnp.concatenate([jnp.where(lowu, u, zero), jnp.where(lowu, zero, u)], axis=0)

    def pick(table, i, j):
        return jnp.where(low, table[i], table[j])

    def two_pairs(base, stage, s):
        bd = [blocks(stage, s), blocks(stage, s + 1)]
        r = [(rows[base + s + e], rows[base + 16 + s + e]) for e in (0, 1)]
        c = [(cols[base + s + e], cols[base + 16 + s + e]) for e in (0, 1)]

        def spread(x):
            return jnp.concatenate([jnp.concatenate([x[0], nothing], axis=1),
                                    jnp.concatenate([nothing, x[1]], axis=1)], axis=0)

        xc = spread([pick(x2c, *c[e]) for e in (0, 1)])
        xr = spread([pick(x2r, *r[e]) for e in (0, 1)])
        fo = lax.dot_general(xc, jnp.concatenate(bd, axis=1), (((1,), (1,)), ((), ())),
                             preferred_element_type=jnp.float32)
        co = lax.dot_general(xr, jnp.concatenate(bd, axis=0), (((1,), (0,)), ((), ())),
                             preferred_element_type=jnp.float32)
        for e in (0, 1):
            f_acc[0][r[e][0]] += fo[16 * e:16 * e + 16]
            f_acc[1][r[e][1]] += fo[16 * e:16 * e + 16]
            c_acc[0][c[e][0]] += co[16 * e:16 * e + 16]
            c_acc[1][c[e][1]] += co[16 * e:16 * e + 16]

    for p in range(32):
        relayout(0, stages[0], p)

    @pl.loop(0, chunks // UNROLL)
    def _(h):
        first = h * UNROLL
        for e in range(UNROLL):
            k = first + e
            nxt = k + 1 if e < UNROLL - 1 else jnp.minimum(k + 1, chunks - 1)
            for s in range(0, 16, 2):
                two_pairs(k * 32, stages[e % 2], s)
                for p in range(2 * s, 2 * s + 4):
                    relayout(nxt, stages[1 - e % 2], p)


def local_products(rows, cols, count, x2r, x2c, tiles, sums):
    smem = pl.BlockSpec(memory_space=pltpu.SMEM)
    vmem = pl.BlockSpec(memory_space=pltpu.VMEM)
    return pl.pallas_call(
        local_kernel,
        out_shape=tuple(jax.ShapeDtypeStruct(v.shape, v.dtype) for v in sums),
        in_specs=[smem] * 3 + [vmem] * 7,
        out_specs=(vmem,) * 4,
        input_output_aliases={6: 0, 7: 1, 8: 2, 9: 3},
        scratch_shapes=[pltpu.VMEM((64 * PITCH, 128), jnp.float32)] * 2,
        compiler_params=pltpu.CompilerParams(vmem_limit_bytes=24 << 20),
        name="local_products",
    )(rows, cols, count, x2r, x2c, tiles, *sums)


def on_device(vectors, tiles, tile_rows, tile_cols, tile_counts):
    x2r, x2c, *sums = gather(pltpu.with_memory_space_constraint(vectors, pltpu.HBM))
    sums = local_products(
        tile_rows.reshape(-1), tile_cols.reshape(-1), tile_counts.reshape(-1),
        x2r, x2c, tiles.reshape(tiles.shape[2:]), sums)
    return scatter(vectors.shape, sums)


def solution(mesh):
    return jax.shard_map(
        on_device,
        mesh=mesh,
        in_specs=(
            P(None, ("row", "col")),
            P("row", "col", None, None),
            P("row", "col", None),
            P("row", "col", None),
            P("row", "col"),
        ),
        out_specs=P(None, ("row", "col")),
        check_vma=False,
    )
```
